32 devices in a mesh: frame: 8 (over z, core), row: 4 (over y, x).
Axes of the slice: x: 2, y: 2, z: 4, core: 2. Of those that a mesh axis runs over, the one named last changes fastest.
Arguments:
- video_frames: bfloat16 [16, 512, 2048], P('frame', 'row'), may hold values from -6 to 6
- split_frames: bfloat16 [16, 512, 2048], P('frame', 'row'), may hold values from -6 to 6
- dual_frames: bfloat16 [16, 512, 2048], P('frame', 'row'), may hold values from -6 to 6
- sensor_image: float32 [512, 2048], P('row'), may hold values from -24 to 24
- kernel_vertical: bfloat16 [2, 768], replicated, may hold values from -0.21875 to 0.21875
- kernel_horizontal: bfloat16 [2, 768], replicated, may hold values from -0.21875 to 0.21875
- shutter_start: int32 [4], replicated, may hold values from 0 to 15, as said below
- shutter_end: int32 [4], replicated, may hold values from 1 to 16
Outputs:
- video_next: bfloat16 [16, 512, 2048], P('frame', 'row')
- split_next: bfloat16 [16, 512, 2048], P('frame', 'row')
- dual_next: bfloat16 [16, 512, 2048], P('frame', 'row')
The draws below stay inside these ranges and needn't reach their ends.
Inputs may be any that keep to these rules, and one draw needn't show every extreme that they name: For every row band j, shutter_start[j] < shutter_end[j]; row band j holds sensor rows j * 128 to (j + 1) * 128 - 1.
All inputs are finite; a program needn't handle non-finite values.
Results may differ from the reference program's by a relative error of at most 0.0095.
Values may be sent and summed in bfloat16 or wider, within the bound.
No kernel may reach another device: no remote copies, remote signals or barrier semaphores. Data moves between devices by JAX's collectives and lax.ppermute only.
A program may use at most 64 MiB of HBM per device.

```python
import jax
import jax.numpy as jnp
from jax import lax

BLOCK = 128
WIDTH = 2048
RANK = 2
TAPS = 768
FRAMES = 16
HEIGHT = 512
BANDS = 4


def shutter_pair(key):
    first_draw = jax.random.randint(jax.random.fold_in(key, 1), (BANDS,), 0, FRAMES, dtype=jnp.int32)
    second_draw = jax.random.randint(jax.random.fold_in(key, 2), (BANDS,), 1, FRAMES + 1, dtype=jnp.int32)
    start_value = jnp.minimum(first_draw, second_draw - 1)
    end_value = jnp.maximum(first_draw + 1, second_draw)
    order = jax.random.permutation(jax.random.fold_in(key, 3), BANDS)
    positions = jnp.arange(BANDS, dtype=jnp.int32)
    start_value = jnp.where(positions == order[0], 0, start_value)
    end_value = jnp.where(positions == order[0], 1, end_value)
    start_value = jnp.where(positions == order[1], FRAMES - 1, start_value)
    end_value = jnp.where(positions == order[1], FRAMES, end_value)
    return (start_value.astype(jnp.int32), end_value.astype(jnp.int32))


def draw_shutter_start(key, part):
    return shutter_pair(key)[0]


def draw_shutter_end(key, part):
    return shutter_pair(key)[1]


def shard_levels(own_key, dims, split, low, top_value):
    level = 1.0
    for position, blocks in split:
        steps = jax.random.uniform(jax.random.fold_in(jax.random.fold_in(own_key, 6), position), (blocks,), jnp.float32, low / len(split), top_value / len(split))
        level = level * jnp.repeat(jnp.exp(steps), dims[position] // blocks).reshape((-1,) + (1,) * (len(dims) - 1 - position))
    return level


def centred(rng, shape, deviation, most, cuts=(), held_as=jnp.bfloat16):
    result = jax.random.normal(rng, shape, jnp.float32) * deviation
    if len(cuts) > 0:
        result = shard_levels(rng, shape, cuts, -0.22, 0.18) * result
    return jnp.clip(result, min=-most, max=most).astype(held_as)


def setup_inputs(seed: int = 0) -> dict:
    key_of = jax.random.split(jax.random.key(seed), 9)
    return {
        "video_frames": centred(key_of[0], (FRAMES, HEIGHT, WIDTH), 1.0, 6.0, ((0, 8), (1, 4))),
        "split_frames": centred(key_of[1], (FRAMES, HEIGHT, WIDTH), 1.0, 6.0, ((0, 8), (1, 4))),
        "dual_frames": centred(key_of[2], (FRAMES, HEIGHT, WIDTH), 1.0, 6.0, ((0, 8), (1, 4))),
        "sensor_image": centred(key_of[3], (HEIGHT, WIDTH), 4.0, 24.0, ((0, 4),), jnp.float32),
        "kernel_vertical": centred(key_of[4], (RANK, TAPS), TAPS ** -0.5, 0.21875),
        "kernel_horizontal": centred(key_of[5], (RANK, TAPS), TAPS ** -0.5, 0.21875),
        "shutter_start": draw_shutter_start(jax.random.fold_in(key_of[8], 71), 0),
        "shutter_end": draw_shutter_end(jax.random.fold_in(key_of[8], 71), 0),
    }


tau_step = 0.1
rho_weight = 2.0


def toeplitz_blocks(kernel, block_rows):
    rank_count = kernel.shape[0]
    padded = jnp.pad(kernel, ((0, 0), (block_rows, block_rows)))
    pieces = jnp.stack([padded[:, block_rows * e + 1:block_rows * e + 2 * block_rows] for e in range(7)], axis=1)
    wrapped = jnp.pad(pieces, ((0, 0), (0, 0), (0, 1)))
    tiled = jnp.tile(wrapped, (1, 1, block_rows))
    shaped = tiled[:, :, :block_rows * (2 * block_rows - 1)].reshape(rank_count, 7, block_rows, 2 * block_rows - 1)
    return shaped[:, :, :, block_rows - 1:2 * block_rows - 1]


def rows_pass(blocks, frame, adjoint):
    height, width_cols = frame.shape
    margin = 3 * BLOCK
    padded = jnp.pad(frame, ((margin, margin), (0, 0)))
    pattern = "rji,pjw->rpiw" if adjoint else "rij,pjw->rpiw"
    summed = jnp.zeros((RANK, height // BLOCK, BLOCK, width_cols), jnp.float32)
    for offset in range(-3, 4):
        begin_row = (3 - offset if adjoint else 3 + offset) * BLOCK
        row_view = padded[begin_row:begin_row + height].reshape(height // BLOCK, BLOCK, width_cols)
        summed = summed + jnp.einsum(pattern, blocks[:, offset + 3].astype(jnp.float32), row_view.astype(jnp.float32))
    return summed.reshape(RANK, height, width_cols)


def columns_pass(blocks, data, adjoint):
    rank_count, row_count, width_cols = data.shape
    margin = 3 * BLOCK
    padded = jnp.pad(data, ((0, 0), (0, 0), (margin, margin)))
    pattern = "rhnj,rji->hni" if adjoint else "rhnj,rij->hni"
    summed = jnp.zeros((row_count, width_cols // BLOCK, BLOCK), jnp.float32)
    for offset in range(-3, 4):
        begin_col = (3 - offset if adjoint else 3 + offset) * BLOCK
        col_view = padded[:, :, begin_col:begin_col + width_cols].reshape(rank_count, row_count, width_cols // BLOCK, BLOCK)
        summed = summed + jnp.einsum(pattern, col_view.astype(jnp.float32), blocks[:, offset + 3].astype(jnp.float32))
    return summed.reshape(row_count, width_cols)


def reference(video_frames, split_frames, dual_frames, sensor_image, kernel_vertical, kernel_horizontal, shutter_start, shutter_end):
    vertical_blocks = toeplitz_blocks(kernel_vertical, BLOCK)
    horizontal_blocks = toeplitz_blocks(kernel_horizontal, BLOCK)
    band_rows = jnp.arange(HEIGHT, dtype=jnp.int32) // BLOCK
    start_rows = shutter_start[band_rows]
    end_rows = shutter_end[band_rows]

    def active_rows(frame_index):
        return (start_rows <= frame_index) & (frame_index < end_rows)

    def accumulate(measured, item):
        frame_index, frame = item
        rowed = rows_pass(vertical_blocks, frame, False).astype(jnp.bfloat16)
        blurred = columns_pass(horizontal_blocks, rowed, False).astype(jnp.bfloat16)
        measured = measured + jnp.where(active_rows(frame_index)[:, None], blurred.astype(jnp.float32), jnp.zeros((), jnp.float32))
        return measured, None

    frame_ids = jnp.arange(FRAMES, dtype=jnp.int32)
    measured, _ = lax.scan(accumulate, jnp.zeros((HEIGHT, WIDTH), jnp.float32), (frame_ids, video_frames))
    residual = (measured - sensor_image).astype(jnp.bfloat16)

    def update(item):
        frame_index, frame, split_frame, dual_frame = item
        masked = jnp.where(active_rows(frame_index)[:, None], residual, jnp.zeros((), jnp.bfloat16))
        back = rows_pass(vertical_blocks, masked, True).astype(jnp.bfloat16)
        gradient = columns_pass(horizontal_blocks, back, True)
        current = frame.astype(jnp.float32)
        dual_value = dual_frame.astype(jnp.float32)
        moved_frames = current - tau_step * (gradient + rho_weight * (current - split_frame.astype(jnp.float32) + dual_value))
        shifted = moved_frames + dual_value
        clamped = jnp.maximum(shifted, 0.0)
        return moved_frames.astype(jnp.bfloat16), clamped.astype(jnp.bfloat16), (shifted - clamped).astype(jnp.bfloat16)

    video_next, split_next, dual_next = lax.map(update, (frame_ids, video_frames, split_frames, dual_frames))
    return (video_next, split_next, dual_next)
```

```python
import functools

import jax
import jax.numpy as jnp
from jax import lax
from jax.experimental import pallas as pl
from jax.experimental.pallas import tpu as pltpu
from jax.sharding import PartitionSpec as P

tau_step = 0.1
rho_weight = 2.0
reach = 3
f32 = jnp.float32
bf16 = jnp.bfloat16
vmem = pl.BlockSpec(memory_space=pltpu.VMEM)
smem = pl.BlockSpec(memory_space=pltpu.SMEM)


def row_steps(count):
    if count <= reach + 1:
        return tuple(range(count))
    return (0, 1, 2, 3, -1, -2, -3)


def band_at(row, step, count):
    if count <= reach + 1:
        return lax.rem(row + step + count, count)
    return row + step


def over_rows(value, step, count):
    if count <= reach + 1:
        pairs = [(i, (i + step) % count) for i in range(count)]
    else:
        pairs = [(i, i + step) for i in range(count) if 0 <= i + step < count]
    return lax.ppermute(value, "row", pairs)


def over_pair(value, count):
    return lax.ppermute(value, "frame", [(i, i ^ 1) for i in range(count)])


def over_groups(value, step, count):
    groups = count // 2
    pairs = [(2 * g + c, 2 * ((g + step) % groups) + c) for g in range(groups) for c in range(2)]
    return lax.ppermute(value, "frame", pairs)


def frame_scale(start_ref, end_ref, band, frame):
    live = (start_ref[band] <= frame) & (frame < end_ref[band])
    return jnp.where(live, 1.0, 0.0).astype(f32)


def sums_kernel(rows, start_ref, end_ref, video_ref, keep_ref, send_ref):
    frames, height, _ = video_ref.shape
    half = height // 2
    place = lax.axis_index("frame")
    core = lax.rem(place, 2)
    row = lax.axis_index("row")
    for which, out_ref in ((core, keep_ref), (1 - core, send_ref)):
        begin = pl.multiple_of(which * half, half)
        data = [video_ref[f, pl.ds(begin, half), :].astype(f32) for f in range(frames)]
        for n, step in enumerate(row_steps(rows)):
            band = jnp.clip(band_at(row, step, rows), 0, rows - 1)
            total = jnp.zeros_like(data[0])
            for f in range(frames):
                total = total + data[f] * frame_scale(start_ref, end_ref, band, place * frames + f)
            out_ref[n] = total.astype(bf16)


def tile_of(chunks_ref, r, e, shift=None):
    block = chunks_ref.shape[-1]
    window = jnp.concatenate(
        [chunks_ref[r, pl.ds(e + 1, 1), :], chunks_ref[r, pl.ds(e, 1), :]], axis=1
    )
    wide = jnp.broadcast_to(window, (block, 2 * block))
    turned = pltpu.roll(wide, 0, 1, stride=1, stride_axis=0)
    if shift is not None:
        turned = pltpu.roll(turned, shift, 1)
    return turned[:, :block]


def weights_kernel(rows, kv_ref, kh_ref, down_ref, up_ref, ahead_ref, behind_ref, cv_ref, ch_ref):
    ranks, taps = kv_ref.shape
    chunks = cv_ref.shape[1]
    block = cv_ref.shape[2]
    core = lax.rem(lax.axis_index("frame"), 2)
    row = lax.axis_index("row")
    steps = row_steps(rows)
    half = block // 2
    for src, dst in ((kv_ref, cv_ref), (kh_ref, ch_ref)):
        data = src[...].astype(f32)
        dst[...] = jnp.zeros_like(dst)
        for e in range(taps // block):
            dst[:, e + 1, :] = data[:, block * e : block * (e + 1)]
    lane = lax.broadcasted_iota(jnp.int32, (block, block), 1)
    down_ref[...] = jnp.zeros_like(down_ref)
    for r in range(ranks):
        parts = []
        for n, step in enumerate(steps):
            gap = band_at(row, -step, rows) - row
            shift = 2 * block - core * half + (n % 2) * half
            parts.append(tile_of(cv_ref, r, gap + reach, lax.rem(shift, 2 * block)))
            up = tile_of(cv_ref, r, reach - gap)
            up_ref[r * block : (r + 1) * block, n * block : (n + 1) * block] = up.T.astype(bf16)
        for n in range(0, len(parts), 2):
            odd = parts[n + 1] if n + 1 < len(parts) else jnp.zeros_like(parts[n])
            both = jnp.where(lane < half, parts[n], odd)
            down_ref[r * block : (r + 1) * block, n * half : n * half + block] = both.astype(bf16)
        deep, wide = ahead_ref.shape[1:]
        tiles = [tile_of(ch_ref, r, e) for e in range(2 * reach + 1)]
        plain = [t.astype(bf16) for t in tiles]
        turned = [t.T.astype(bf16) for t in tiles]
        empty = jnp.zeros((block, block), bf16)
        for a in range(deep // block):
            for b in range(wide // block):
                where = (r, slice(a * block, (a + 1) * block), slice(b * block, (b + 1) * block))
                e = a - b
                ahead_ref[where] = turned[e] if 0 <= e <= 2 * reach else empty
                e = 2 * reach + b - a
                behind_ref[where] = plain[e] if 0 <= e <= 2 * reach else empty


def dot(a, b):
    return jnp.dot(a, b, preferred_element_type=f32)


def blur_kernel(count, *refs):
    pieces = refs[:count]
    down_ref, ahead_ref, keep_ref, send_ref, stack, padded, total = refs[count:]
    half, width = keep_ref.shape
    height = 2 * half
    ranks, deep, wide = ahead_ref.shape
    margin = reach * height
    core = lax.rem(lax.axis_index("frame"), 2)
    if stack.shape[0] > count * half:
        stack[count * half :, :] = jnp.zeros((stack.shape[0] - count * half, width), bf16)
    for n in range(count):
        stack[n * half : (n + 1) * half, :] = pieces[n][...]
    for r in range(ranks):
        padded[r, :, :margin] = jnp.zeros((height, margin), bf16)
        padded[r, :, margin + width :] = jnp.zeros((height, margin), bf16)
        for x in range(0, width, 512):
            padded[r, :, margin + x : margin + x + 512] = dot(
                down_ref[r * height : (r + 1) * height, :], stack[:, x : x + 512]
            ).astype(bf16)
    for x in range(0, width, wide):
        acc = dot(padded[0, :, x : x + deep], ahead_ref[0])
        for r in range(1, ranks):
            acc = acc + dot(padded[r, :, x : x + deep], ahead_ref[r])
        total[:, x : x + wide] = acc
    keep_ref[...] = total[pl.ds(pl.multiple_of(core * half, half), half), :]
    send_ref[...] = total[pl.ds(pl.multiple_of((1 - core) * half, half), half), :].astype(bf16)


def split_kernel(groups, keep_ref, recv_ref, *refs):
    outs, total = refs[:groups], refs[groups]
    rows = outs[0].shape[0]
    group = lax.axis_index("frame") // 2
    total[...] = keep_ref[...] + recv_ref[...].astype(f32)
    for step in range(groups):
        begin = pl.multiple_of(lax.rem(group + step, groups) * rows, rows)
        outs[step][...] = total[pl.ds(begin, rows), :].astype(outs[step].dtype)


def join_kernel(groups, *refs):
    pieces, out_ref, held = refs[:groups], refs[groups], refs[groups + 1]
    rows = pieces[0].shape[0]
    group = lax.axis_index("frame") // 2
    for step in range(groups):
        begin = pl.multiple_of(lax.rem(group - step + groups, groups) * rows, rows)
        held[pl.ds(begin, rows), :] = pieces[step][...].astype(f32)
    out_ref[...] = held[...].astype(bf16)


def update_kernel(rows, count, start_ref, end_ref, *refs):
    own, other = refs[:count], refs[count : 2 * count]
    up_ref, behind_ref, video_ref, split_ref, dual_ref = refs[2 * count : 2 * count + 5]
    video_out, split_out, dual_out, stack, padded = refs[2 * count + 5 :]
    half, width = own[0].shape
    height = 2 * half
    ranks, deep, wide = behind_ref.shape
    frames = video_ref.shape[0]
    margin = reach * height
    place = lax.axis_index("frame")
    core = lax.rem(place, 2)
    row = lax.axis_index("row")
    block = pl.program_id(0)

    @pl.when(block == 0)
    def _():
        for n in range(count):
            for which, src in ((core, own[n]), (1 - core, other[n])):
                begin = pl.multiple_of(n * height + which * half, half)
                stack[pl.ds(begin, half), :] = src[...]
        for r in range(ranks):
            padded[r, :, :margin] = jnp.zeros((frames * height, margin), bf16)
            padded[r, :, margin + width :] = jnp.zeros((frames * height, margin), bf16)
        for f in range(frames):
            masked = []
            for n, step in enumerate(row_steps(rows)):
                band = jnp.clip(band_at(row, -step, rows), 0, rows - 1)
                scale = frame_scale(start_ref, end_ref, band, place * frames + f)
                part = up_ref[:, n * height : (n + 1) * height].astype(f32) * scale
                masked.append(part.astype(bf16))
            weights = jnp.concatenate(masked, axis=1)
            for x in range(0, width, 512):
                back = dot(weights, stack[:, x : x + 512]).astype(bf16)
                for r in range(ranks):
                    padded[r, f * height : (f + 1) * height, margin + x : margin + x + 512] = back[
                        r * height : (r + 1) * height, :
                    ]

    begin = pl.multiple_of(block * wide, wide)
    gradient = dot(padded[0, :, pl.ds(begin, deep)], behind_ref[0])
    for r in range(1, ranks):
        gradient = gradient + dot(padded[r, :, pl.ds(begin, deep)], behind_ref[r])
    for f in range(frames):
        current = video_ref[f].astype(f32)
        dual_value = dual_ref[f].astype(f32)
        moved = current - tau_step * (
            gradient[f * height : (f + 1) * height, :]
            + rho_weight * (current - split_ref[f].astype(f32) + dual_value)
        )
        shifted = moved + dual_value
        clamped = jnp.maximum(shifted, 0.0)
        video_out[f] = moved.astype(bf16)
        split_out[f] = clamped.astype(bf16)
        dual_out[f] = (shifted - clamped).astype(bf16)


def cost(flops, moved):
    return pl.CostEstimate(flops=flops, bytes_accessed=moved, transcendentals=0)


def per_device(places, rows, video, split, dual, sensor, kv, kh, start, end):
    frames, height, width = video.shape
    half = height // 2
    ranks, taps = kv.shape
    groups = places // 2
    slab = half // groups
    steps = row_steps(rows)
    count = len(steps)
    wide = 2 * height
    deep = wide + 2 * reach * height
    stacked = (count + count % 2) * half
    shape = jax.ShapeDtypeStruct
    params = pltpu.CompilerParams(vmem_limit_bytes=48 << 20)

    keep, send = pl.pallas_call(
        functools.partial(sums_kernel, rows),
        grid=(4,),
        out_shape=[shape((count, half, width), bf16)] * 2,
        in_specs=[smem, smem, pl.BlockSpec((frames, height, width // 4), lambda i: (0, 0, i))],
        out_specs=[pl.BlockSpec((count, half, width // 4), lambda i: (0, 0, i))] * 2,
        cost_estimate=cost(4 * count * video.size, 6 * video.size),
        compiler_params=params,
        name="frame_sums",
    )(start, end, video)
    recv = over_pair(send, places)
    sums = [(keep[n].astype(f32) + recv[n].astype(f32)).astype(bf16) for n in range(count)]
    pieces = [sums[0]] + [over_rows(sums[n], steps[n], rows) for n in range(1, count)]

    down, up, ahead, behind = pl.pallas_call(
        functools.partial(weights_kernel, rows),
        out_shape=[
            shape((ranks * height, stacked), bf16),
            shape((ranks * height, count * height), bf16),
            shape((ranks, deep, wide), bf16),
            shape((ranks, deep, wide), bf16),
        ],
        in_specs=[vmem, vmem],
        out_specs=[vmem] * 4,
        scratch_shapes=[pltpu.VMEM((ranks, taps // height + 2, height), f32)] * 2,
        cost_estimate=cost(1 << 22, 4 << 20),
        compiler_params=params,
        name="toeplitz",
    )(kv, kh)

    keep, send = pl.pallas_call(
        functools.partial(blur_kernel, count),
        out_shape=[shape((half, width), f32), shape((half, width), bf16)],
        in_specs=[vmem] * (count + 2),
        out_specs=[vmem] * 2,
        scratch_shapes=[
            pltpu.VMEM((stacked, width), bf16),
            pltpu.VMEM((ranks, height, width + 2 * reach * height), bf16),
            pltpu.VMEM((height, width), f32),
        ],
        cost_estimate=cost(2 * ranks * height * width * (stacked + deep), 4 << 20),
        compiler_params=params,
        name="blur",
    )(*pieces, down, ahead)
    recv = over_pair(send, places)

    parts = pl.pallas_call(
        functools.partial(split_kernel, groups),
        out_shape=[shape((slab, width), f32)] + [shape((slab, width), bf16)] * (groups - 1),
        in_specs=[vmem] * 2,
        out_specs=[vmem] * groups,
        scratch_shapes=[pltpu.VMEM((half, width), f32)],
        cost_estimate=cost(half * width, 1 << 20),
        compiler_params=params,
        name="split_rows",
    )(keep, recv)
    place = lax.axis_index("frame")
    begin = lax.rem(place, 2) * half + (place // 2) * slab
    total = parts[0] - lax.dynamic_slice_in_dim(sensor, begin, slab, 0)
    for step in range(1, groups):
        total = total + over_groups(parts[step], step, places).astype(f32)
    residual = total.astype(bf16)

    gathered = [residual] + [over_groups(residual, step, places) for step in range(1, groups)]
    band = pl.pallas_call(
        functools.partial(join_kernel, groups),
        out_shape=shape((half, width), bf16),
        in_specs=[vmem] * groups,
        out_specs=vmem,
        scratch_shapes=[pltpu.VMEM((half, width), f32)],
        cost_estimate=cost(half * width, 1 << 20),
        compiler_params=params,
        name="join_rows",
    )(*gathered)
    own = [band] + [over_rows(band, step, rows) for step in steps[1:]]
    other = [over_pair(piece, places) for piece in own]

    column = pl.BlockSpec((frames, height, wide), lambda i: (0, 0, i))
    return pl.pallas_call(
        functools.partial(update_kernel, rows, count),
        grid=(width // wide,),
        out_shape=[shape(video.shape, bf16)] * 3,
        in_specs=[smem, smem] + [vmem] * (2 * count + 2) + [column] * 3,
        out_specs=[column] * 3,
        scratch_shapes=[
            pltpu.VMEM((count * height, width), bf16),
            pltpu.VMEM((ranks, frames * height, width + 2 * reach * height), bf16),
        ],
        cost_estimate=cost(2 * ranks * frames * height * width * (count * height + deep), 8 << 20),
        compiler_params=params,
        name="update",
    )(start, end, *own, *other, up, behind, video, split, dual)


def solution(mesh):
    stacked = P("frame", "row", None)
    return jax.shard_map(
        functools.partial(per_device, mesh.shape["frame"], mesh.shape["row"]),
        mesh=mesh,
        in_specs=(stacked, stacked, stacked, P("row", None), P(), P(), P(), P()),
        out_specs=(stacked, stacked, stacked),
        check_vma=False,
    )
```
